32 devices in a mesh: wide: 8 (over y, x, core), narrow: 4 (over z).
Axes of the slice: x: 2, y: 2, z: 4, core: 2. Of those that a mesh axis runs over, the one named last changes fastest.
Arguments:
- trajectory: bfloat16 [5, 72, 256, 1024], P(None, None, 'narrow', 'wide'), may hold values from -6 to 6
- innovation: float32 [5, 72, 64, 256], P(None, None, 'narrow', 'wide'), may hold values from -6 to 6
- background: float32 [5, 72, 64, 256], P(None, None, 'narrow', 'wide'), may hold values from -6 to 6
- obs_weight: float32 [72, 64, 256], P(None, 'narrow', 'wide'), may hold values from 0.3 to 3
Outputs:
- analysis: bfloat16 [5, 72, 256, 1024], P(None, None, 'narrow', 'wide')
The draws below stay inside these ranges and needn't reach their ends.
All inputs are finite; a program needn't handle non-finite values.
Results may differ from the reference program's by a relative error of at most 0.001.
Values sent between devices are 32-bit elements; how exact they have to be, the bound alone decides.
A program may use at most 128 MiB of HBM per device.

```python
import math
import jax
import jax.numpy as jnp
from jax import lax

FIELDS = 5
LEVELS = 72
COARSEN = 4
STEPS = 2
ITERS = 1
NLAT = 256
NLON = 1024
NLAT_C = 64
NLON_C = 256


def levels(stream_key, dims, pieces, least, largest):
    factor_of = 1.0
    for axis_at, blocks in pieces:
        draws = jax.random.uniform(jax.random.fold_in(jax.random.fold_in(stream_key, 6), axis_at), (blocks,), jnp.float32, least / len(pieces), largest / len(pieces))
        factor_of = factor_of * jnp.repeat(jnp.exp(draws), dims[axis_at] // blocks).reshape((-1,) + (1,) * (len(dims) - 1 - axis_at))
    return factor_of


def normal_values(rng, extent, deviation, most, split=(), kind=jnp.bfloat16):
    level = levels(rng, extent, split, -0.22, 0.18) if split else 1.0
    drawn = jax.random.normal(rng, extent, jnp.float32) * deviation * level
    return jnp.minimum(jnp.maximum(drawn, -most), most).astype(kind)


def setup_inputs(seed: int = 0) -> dict:
    arg_keys = jax.random.split(jax.random.key(seed), 5)
    return {
        "trajectory": normal_values(arg_keys[0], (FIELDS, LEVELS, NLAT, NLON), 1.0, 6.0, ((2, 4), (3, 8))),
        "innovation": normal_values(arg_keys[1], (FIELDS, LEVELS, NLAT_C, NLON_C), 1.0, 6.0, ((2, 4), (3, 8)), jnp.float32),
        "background": normal_values(arg_keys[2], (FIELDS, LEVELS, NLAT_C, NLON_C), 0.7, 6.0, ((2, 4), (3, 8)), jnp.float32),
        "obs_weight": jnp.clip(jnp.exp(math.log(3.0) - 2.3025851 * jax.random.uniform(arg_keys[3], (LEVELS, NLAT_C, NLON_C), jnp.float32) ** levels(arg_keys[3], (LEVELS, NLAT_C, NLON_C), ((1, 4), (2, 8)), -0.2, 0.2)), 0.3, 3.0),
    }


diffusion = 0.2
advection_scale = 0.3
descent_step = 1.0


def filter_rows(row_index, total_rows, cycle_size):
    wavenumber = jnp.arange(cycle_size, dtype=jnp.int32)
    folded = jnp.minimum(wavenumber, cycle_size - wavenumber).astype(jnp.float32)
    latitude = jnp.pi * ((row_index.astype(jnp.float32) + 0.5) / total_rows - 0.5)
    cutoff = 0.5 * cycle_size * jnp.cos(latitude)
    scaled_wave = folded[None, :] / cutoff[:, None]
    response = 1.0 / (1.0 + scaled_wave ** 4)
    phase_index = (wavenumber[:, None] * wavenumber[None, :]) % cycle_size
    angles = (2.0 * jnp.pi / cycle_size) * phase_index.astype(jnp.float32)
    basis = jnp.concatenate([jnp.cos(angles), jnp.sin(angles)], axis=0)
    doubled = jnp.concatenate([response, response], axis=1)
    weighted = doubled[:, :, None] * basis[None]
    return jnp.einsum("rka,kb->rab", weighted, basis, precision=lax.Precision.HIGHEST) / cycle_size


def tangent_step(model_state, extend_rows, drift_coef, kernel):
    padded = extend_rows(model_state)
    north_row = padded[:, :, :-2]
    south_row = padded[:, :, 2:]
    east_cell = jnp.roll(model_state, -1, axis=3)
    west_cell = jnp.roll(model_state, 1, axis=3)
    updated = model_state + diffusion * (north_row + south_row + east_cell + west_cell - 4.0 * model_state) + drift_coef * (east_cell - west_cell)
    return jnp.einsum("flrb,rbc->flrc", updated, kernel, precision=lax.Precision.HIGHEST)


def adjoint_step(costate, extend_rows, drift_coef, kernel):
    filtered = jnp.einsum("flrb,rbc->flrc", costate, kernel, precision=lax.Precision.HIGHEST)
    padded = extend_rows(filtered)
    north_row = padded[:, :, :-2]
    south_row = padded[:, :, 2:]
    east_cell = jnp.roll(filtered, -1, axis=3)
    west_cell = jnp.roll(filtered, 1, axis=3)
    carried = drift_coef * filtered
    return filtered + diffusion * (north_row + south_row + east_cell + west_cell - 4.0 * filtered) + jnp.roll(carried, 1, axis=3) - jnp.roll(carried, -1, axis=3)


def pad_rows(model_state):
    return jnp.pad(model_state, ((0, 0), (0, 0), (1, 1), (0, 0)))


def reference(trajectory, innovation, background, obs_weight):
    coarse_rows = NLAT_C
    cycle_size = NLON_C
    zonal_wind = trajectory[0].astype(jnp.float32).reshape(LEVELS, coarse_rows, COARSEN, cycle_size, COARSEN)
    zonal_wind = jnp.mean(zonal_wind, axis=(2, 4))
    drift_coef = (advection_scale * jnp.tanh(zonal_wind))[None]
    kernel = filter_rows(jnp.arange(coarse_rows, dtype=jnp.int32), coarse_rows, cycle_size)
    increment = background
    for outer_turn in range(ITERS):
        model_state = increment
        for step_index in range(STEPS):
            model_state = tangent_step(model_state, pad_rows, drift_coef, kernel)
        costate = obs_weight[None] * (model_state - innovation)
        for step_index in range(STEPS):
            costate = adjoint_step(costate, pad_rows, drift_coef, kernel)
        increment = increment - descent_step * (increment - background + costate)

    def finish(field_pair):
        layer_field, coarse_part = field_pair
        fine_part = jnp.repeat(jnp.repeat(coarse_part, COARSEN, axis=2), COARSEN, axis=1)
        return (layer_field.astype(jnp.float32) + fine_part).astype(jnp.bfloat16)

    return lax.map(finish, (trajectory, increment))
```

```python
import functools

import jax
import jax.numpy as jnp
import numpy as np
from jax import lax
from jax.experimental import pallas as pl
from jax.experimental.pallas import tpu as pltpu
from jax.sharding import PartitionSpec as P

MESH = pl.DeviceIdType.MESH
FIELDS = 5
COARSEN = 4
STEPS = 2
LANES = 128
HALO = 2 * STEPS
ITEMS = 2 * FIELDS + 2

diffusion = 0.2
advection_scale = 0.3
descent_step = 1.0


def split_bf16(x):
    high = x.astype(jnp.bfloat16)
    low = (x - high.astype(jnp.float32)).astype(jnp.bfloat16)
    return high, low


def dot(a, b):
    return jnp.dot(a, b, preferred_element_type=jnp.float32)


def block_transpose(tiles, block):
    lane = lax.broadcasted_iota(jnp.int32, tiles[0].shape, len(tiles[0].shape) - 1) // block
    axis = len(tiles[0].shape) - 1
    tiles = list(tiles)
    for step in (2, 1):
        upper = (lane // step) % 2 == 1
        for first in range(4):
            if (first // step) % 2 == 0:
                second = first + step
                a, b = tiles[first], tiles[second]
                tiles[first] = jnp.where(upper, pltpu.roll(b, step * block, axis), a)
                tiles[second] = jnp.where(upper, b, pltpu.roll(a, LANES - step * block, axis))
    return tiles


def pack_kernel(traj_ref, depart_ref, back_ref, weight_ref, pool_ref, out_ref, sums):
    levels, fine_rows, fine_cols = traj_ref.shape[1:]
    rows = fine_rows // COARSEN
    cols = fine_cols // COARSEN
    sums[...] = dot(traj_ref[0].reshape(levels * fine_rows, fine_cols), pool_ref[...])
    total = sums[pl.ds(0, levels * rows, stride=COARSEN), :]
    for t in range(1, COARSEN):
        total = total + sums[pl.ds(t, levels * rows, stride=COARSEN), :]
    drift = advection_scale * jnp.tanh(total * (1.0 / (COARSEN * COARSEN)))
    drift = drift[:, :cols].reshape(levels, rows, cols)
    items = [back_ref[f] for f in range(FIELDS)] + [drift, weight_ref[...]]
    items += [depart_ref[f] for f in range(FIELDS)]
    for group in range(ITEMS // 4):
        out_ref[:, group] = jnp.concatenate(items[4 * group : 4 * group + 4], axis=-1)


def stencil(q, drift):
    rows, cycle = q.shape[-2:]
    north = pltpu.roll(q, 1, q.ndim - 2)
    south = pltpu.roll(q, rows - 1, q.ndim - 2)
    east = pltpu.roll(q, cycle - 1, q.ndim - 1)
    west = pltpu.roll(q, 1, q.ndim - 1)
    return q + diffusion * (north + south + east + west - 4.0 * q) + drift * (east - west)


def stencil_transposed(g, drift):
    rows, cycle = g.shape[-2:]
    north = pltpu.roll(g, 1, g.ndim - 2)
    south = pltpu.roll(g, rows - 1, g.ndim - 2)
    east = pltpu.roll(g, cycle - 1, g.ndim - 1)
    west = pltpu.roll(g, 1, g.ndim - 1)
    carried = drift * g
    return (
        g
        + diffusion * (north + south + east + west - 4.0 * g)
        + pltpu.roll(carried, 1, g.ndim - 1)
        - pltpu.roll(carried, cycle - 1, g.ndim - 1)
    )


def sweep_kernel(
    wide_count, narrow_count, levels, chunk,
    x_ref, response_ref, wave_high_ref, wave_low_ref, out_ref,
    landed, fields, result, outgoing, up_out, down_out, up_in, down_in,
    local_sem, send_sem, recv_sem, halo_send, halo_recv, back_send, back_recv,
):
    me = lax.axis_index("wide")
    band = lax.axis_index("narrow")
    has_above = band > 0
    has_below = band < narrow_count - 1
    rows = landed.shape[2]
    cycle = fields.shape[2]
    half = cycle // 2
    cols = cycle // wide_count
    padded = fields.shape[1]
    groups = out_ref.shape[1]

    barrier = pltpu.get_barrier_semaphore()
    for k in range(1, wide_count):
        pl.semaphore_signal(
            barrier, inc=1, device_id=(lax.rem(me + k, wide_count), band), device_id_type=MESH
        )

    @pl.when(has_above)
    def _():
        pl.semaphore_signal(barrier, inc=1, device_id=(me, band - 1), device_id_type=MESH)

    @pl.when(has_below)
    def _():
        pl.semaphore_signal(barrier, inc=1, device_id=(me, band + 1), device_id_type=MESH)

    keep = pltpu.make_async_copy(x_ref.at[me], landed.at[me], local_sem.at[0])
    keep.start()
    neighbours = has_above.astype(jnp.int32) + has_below.astype(jnp.int32)
    pl.semaphore_wait(barrier, wide_count - 1 + neighbours)

    sends = []
    for k in range(1, wide_count):
        peer = lax.rem(me + k, wide_count)
        copy = pltpu.make_async_remote_copy(
            src_ref=x_ref.at[peer],
            dst_ref=landed.at[me],
            send_sem=send_sem.at[k],
            recv_sem=recv_sem.at[k],
            device_id=(peer, band),
            device_id_type=MESH,
        )
        copy.start()
        sends.append(copy)
    keep.wait()
    for copy in sends:
        copy.wait_recv()

    low_half = lax.broadcasted_iota(jnp.int32, (8, half), 0) < HALO

    def unpack(level, carry):
        for group in range(ITEMS // 4):
            for tile in range(cycle // LANES):
                got = [landed[4 * tile + m, level * (ITEMS // 4) + group] for m in range(4)]
                for j, value in enumerate(block_transpose(got, cols)):
                    fields[level * ITEMS + 4 * group + j, 0:rows, tile * LANES : (tile + 1) * LANES] = value
        for item in range(ITEMS):
            at = level * ITEMS + item
            top = fields[at, 0:8]
            bottom = fields[at, rows - 8 : rows]
            up_out[at] = jnp.where(low_half, top[:, :half], pltpu.roll(top[:, half:], HALO, 0))
            down_out[at] = jnp.where(low_half, pltpu.roll(bottom[:, :half], HALO, 0), bottom[:, half:])
        return carry

    lax.fori_loop(0, levels, unpack, 0)

    up_copy = pltpu.make_async_remote_copy(
        src_ref=up_out, dst_ref=up_in, send_sem=halo_send.at[0], recv_sem=halo_recv.at[0],
        device_id=(me, band - 1), device_id_type=MESH,
    )
    down_copy = pltpu.make_async_remote_copy(
        src_ref=down_out, dst_ref=down_in, send_sem=halo_send.at[1], recv_sem=halo_recv.at[1],
        device_id=(me, band + 1), device_id_type=MESH,
    )

    @pl.when(has_above)
    def _():
        up_copy.start()

    @pl.when(has_below)
    def _():
        down_copy.start()

    @pl.when(jnp.logical_not(has_below))
    def _():
        up_in[...] = jnp.zeros_like(up_in)

    @pl.when(jnp.logical_not(has_above))
    def _():
        down_in[...] = jnp.zeros_like(down_in)

    @pl.when(has_below)
    def _():
        up_copy.wait_recv()

    @pl.when(has_above)
    def _():
        down_copy.wait_recv()

    def take_halo(level, carry):
        for item in range(ITEMS):
            at = level * ITEMS + item
            below, above = up_in[at], down_in[at]
            fields[at, rows:padded, 0:half] = jnp.where(low_half, below, pltpu.roll(above, HALO, 0))
            fields[at, rows:padded, half:cycle] = jnp.where(low_half, pltpu.roll(below, HALO, 0), above)
        return carry

    lax.fori_loop(0, levels, take_halo, 0)

    def zonal(q):
        shape = q.shape
        high, low = split_bf16(q.reshape(-1, cycle))
        wave_high, wave_low = wave_high_ref[...], wave_low_ref[...]
        spectrum = dot(high, wave_high) + dot(low, wave_high) + dot(high, wave_low)
        spectrum = spectrum.reshape(shape) * response_ref[...]
        high, low = split_bf16(spectrum.reshape(-1, cycle))
        return (dot(high, wave_high) + dot(low, wave_high) + dot(high, wave_low)).reshape(shape)

    def sweep(turn, carry):
        at = turn * chunk
        block = fields[pl.ds(at * ITEMS, chunk * ITEMS)].reshape(chunk, ITEMS, padded, cycle)
        background = block[:, :FIELDS]
        drift = block[:, FIELDS : FIELDS + 1]
        weight = block[:, FIELDS + 1 : FIELDS + 2]
        departure = block[:, FIELDS + 2 :]
        state = background
        for _ in range(STEPS):
            state = zonal(stencil(state, drift))
        costate = weight * (state - departure)
        for _ in range(STEPS):
            costate = stencil_transposed(zonal(costate), drift)
        increment = background - descent_step * ((background - background) + costate)
        result[pl.ds(at * FIELDS, chunk * FIELDS)] = increment.reshape(chunk * FIELDS, padded, cycle)[:, :rows]
        return carry

    lax.fori_loop(0, levels // chunk, sweep, 0)

    def repack(group, carry):
        for tile in range(cycle // LANES):
            parts = [result[4 * group + j, :, tile * LANES : (tile + 1) * LANES] for j in range(4)]
            for m, value in enumerate(block_transpose(parts, cols)):
                outgoing[4 * tile + m, group] = value
        return carry

    lax.fori_loop(0, groups, repack, 0)

    keep_back = pltpu.make_async_copy(outgoing.at[me], out_ref.at[me], local_sem.at[1])
    keep_back.start()
    backs = []
    for k in range(1, wide_count):
        peer = lax.rem(me + k, wide_count)
        copy = pltpu.make_async_remote_copy(
            src_ref=outgoing.at[peer],
            dst_ref=out_ref.at[me],
            send_sem=back_send.at[k],
            recv_sem=back_recv.at[k],
            device_id=(peer, band),
            device_id_type=MESH,
        )
        copy.start()
        backs.append(copy)
    for copy in sends:
        copy.wait_send()

    @pl.when(has_above)
    def _():
        up_copy.wait_send()

    @pl.when(has_below)
    def _():
        down_copy.wait_send()

    keep_back.wait()
    for copy in backs:
        copy.wait()


def finish_kernel(traj_ref, inc_ref, spread_ref, out_ref, wide, tall):
    fields, levels, fine_rows, fine_cols = traj_ref.shape
    groups, rows = inc_ref.shape[1:3]
    high, low = split_bf16(inc_ref[0].reshape(groups * rows, LANES))
    wide[...] = dot(high, spread_ref[...]) + dot(low, spread_ref[...])
    for level in range(levels):
        for f in range(fields):
            item = level * fields + f
            group, j = divmod(item, 4)
            part = wide[group * rows : (group + 1) * rows, j * LANES : (j + 1) * LANES]
            for t in range(COARSEN):
                tall[item, pl.ds(t, rows, stride=COARSEN), :] = part
            out_ref[f, level] = (traj_ref[f, level].astype(jnp.float32) + tall[item]).astype(jnp.bfloat16)


def shards(trajectory, innovation, background, obs_weight):
    wide_count = lax.axis_size("wide")
    narrow_count = lax.axis_size("narrow")
    narrow_index = lax.axis_index("narrow")
    fields, total_levels, rows, cols = innovation.shape
    fine_rows, fine_cols = trajectory.shape[2:]
    cycle = cols * wide_count
    total_rows = rows * narrow_count
    levels = -(-total_levels // wide_count)
    last = -(-total_levels // levels) - 1
    chunk = max(c for c in range(1, 6) if levels % c == 0)
    packed = ITEMS // 4
    groups = -(-fields * levels // 4)
    padded = rows + 2 * HALO

    lane = np.arange(fine_cols)
    pool = np.zeros((fine_cols, LANES), np.float32)
    pool[lane, lane // COARSEN] = 1.0
    spread = np.zeros((LANES, 4 * LANES), np.float32)
    for j in range(4):
        spread[j * cols + lane // COARSEN, j * LANES + lane] = 1.0
    pool = jnp.asarray(pool, jnp.bfloat16)
    spread = jnp.asarray(spread, jnp.bfloat16)

    sent = pl.pallas_call(
        pack_kernel,
        grid=(wide_count,),
        in_specs=[
            pl.BlockSpec((1, levels, fine_rows, fine_cols), lambda s: (0, jnp.minimum(s, last), 0, 0)),
            pl.BlockSpec((fields, levels, rows, cols), lambda s: (0, jnp.minimum(s, last), 0, 0)),
            pl.BlockSpec((fields, levels, rows, cols), lambda s: (0, jnp.minimum(s, last), 0, 0)),
            pl.BlockSpec((levels, rows, cols), lambda s: (jnp.minimum(s, last), 0, 0)),
            pl.BlockSpec((fine_cols, LANES), lambda s: (0, 0)),
        ],
        out_specs=pl.BlockSpec((levels, packed, rows, LANES), lambda s: (s, 0, 0, 0)),
        out_shape=jax.ShapeDtypeStruct((wide_count * levels, packed, rows, LANES), jnp.float32),
        scratch_shapes=[pltpu.VMEM((levels * fine_rows, LANES), jnp.float32)],
        name="pack",
    )(trajectory, innovation, background, obs_weight, pool)
    sent = sent.reshape(wide_count, levels * packed, rows, LANES)

    place = jnp.arange(padded, dtype=jnp.int32)
    row_index = jnp.where(place < rows + HALO, place, place - padded) + narrow_index * rows
    wavenumber = jnp.arange(cycle, dtype=jnp.int32)
    folded = jnp.minimum(wavenumber, cycle - wavenumber).astype(jnp.float32)
    latitude = jnp.pi * ((row_index.astype(jnp.float32) + 0.5) / total_rows - 0.5)
    cutoff = 0.5 * cycle * jnp.cos(latitude)
    inside = (row_index >= 0) & (row_index < total_rows)
    cutoff = jnp.where(inside, cutoff, 1.0)
    response = 1.0 / (1.0 + (folded[None, :] / cutoff[:, None]) ** 4)
    response = jnp.where(inside[:, None], response, 0.0) / cycle

    phase = np.arange(cycle)[:, None] * np.arange(cycle)[None, :] % cycle
    wave = np.cos(2.0 * np.pi / cycle * phase) + np.sin(2.0 * np.pi / cycle * phase)
    wave = wave.astype(np.float32)
    wave_high = wave.astype(jnp.bfloat16)
    wave_low = (wave - wave_high.astype(np.float32)).astype(jnp.bfloat16)

    vmem = pl.BlockSpec(memory_space=pltpu.VMEM)
    anywhere = pl.BlockSpec(memory_space=pl.ANY)
    f32 = jnp.float32
    moved_back = pl.pallas_call(
        functools.partial(sweep_kernel, wide_count, narrow_count, levels, chunk),
        in_specs=[anywhere, vmem, vmem, vmem],
        out_specs=anywhere,
        out_shape=jax.ShapeDtypeStruct((wide_count, groups, rows, LANES), f32),
        scratch_shapes=[
            pltpu.VMEM((wide_count, levels * packed, rows, LANES), f32),
            pltpu.VMEM((levels * ITEMS, padded, cycle), f32),
            pltpu.VMEM((groups * 4, rows, cycle), f32),
            pltpu.VMEM((wide_count, groups, rows, LANES), f32),
            pltpu.VMEM((levels * ITEMS, 8, cycle // 2), f32),
            pltpu.VMEM((levels * ITEMS, 8, cycle // 2), f32),
            pltpu.VMEM((levels * ITEMS, 8, cycle // 2), f32),
            pltpu.VMEM((levels * ITEMS, 8, cycle // 2), f32),
            pltpu.SemaphoreType.DMA((2,)),
            pltpu.SemaphoreType.DMA((wide_count,)),
            pltpu.SemaphoreType.DMA((wide_count,)),
            pltpu.SemaphoreType.DMA((2,)),
            pltpu.SemaphoreType.DMA((2,)),
            pltpu.SemaphoreType.DMA((wide_count,)),
            pltpu.SemaphoreType.DMA((wide_count,)),
        ],
        compiler_params=pltpu.CompilerParams(collective_id=0, has_side_effects=True),
        name="sweep",
    )(sent, response, jnp.asarray(wave_high), jnp.asarray(wave_low))

    return pl.pallas_call(
        finish_kernel,
        grid=(last + 1,),
        in_specs=[
            pl.BlockSpec((fields, levels, fine_rows, fine_cols), lambda s: (0, s, 0, 0)),
            pl.BlockSpec((1, groups, rows, LANES), lambda s: (s, 0, 0, 0)),
            pl.BlockSpec((LANES, 4 * LANES), lambda s: (0, 0)),
        ],
        out_specs=pl.BlockSpec((fields, levels, fine_rows, fine_cols), lambda s: (0, s, 0, 0)),
        out_shape=jax.ShapeDtypeStruct(trajectory.shape, jnp.bfloat16),
        scratch_shapes=[
            pltpu.VMEM((groups * rows, 4 * LANES), f32),
            pltpu.VMEM((fields * levels, fine_rows, fine_cols), f32),
        ],
        name="finish",
    )(trajectory, moved_back, spread)


def solution(mesh):
    in_specs = (
        P(None, None, "narrow", "wide"),
        P(None, None, "narrow", "wide"),
        P(None, None, "narrow", "wide"),
        P(None, "narrow", "wide"),
    )
    out_specs = P(None, None, "narrow", "wide")
    return jax.shard_map(shards, mesh=mesh, in_specs=in_specs, out_specs=out_specs, check_vma=False)
```

```python
import functools

import jax
import jax.numpy as jnp
import numpy as np
from jax import lax
from jax.experimental import pallas as pl
from jax.experimental.pallas import tpu as pltpu
from jax.sharding import PartitionSpec as P

MESH = pl.DeviceIdType.MESH
FIELDS = 5
COARSEN = 4
STEPS = 2
LANES = 128
HALO = 2 * STEPS
ITEMS = 2 * FIELDS + 2

diffusion = 0.2
advection_scale = 0.3
descent_step = 1.0


def split_bf16(x):
    high = x.astype(jnp.bfloat16)
    low = (x - high.astype(jnp.float32)).astype(jnp.bfloat16)
    return high, low


def dot(a, b):
    return jnp.dot(a, b, preferred_element_type=jnp.float32)


def block_transpose(tiles, block):
    lane = lax.broadcasted_iota(jnp.int32, tiles[0].shape, len(tiles[0].shape) - 1) // block
    axis = len(tiles[0].shape) - 1
    tiles = list(tiles)
    for step in (2, 1):
        upper = (lane // step) % 2 == 1
        for first in range(4):
            if (first // step) % 2 == 0:
                second = first + step
                a, b = tiles[first], tiles[second]
                tiles[first] = jnp.where(upper, pltpu.roll(b, step * block, axis), a)
                tiles[second] = jnp.where(upper, b, pltpu.roll(a, LANES - step * block, axis))
    return tiles


def pack_kernel(traj_ref, depart_ref, back_ref, weight_ref, pool_ref, out_ref, sums):
    levels, fine_rows, fine_cols = traj_ref.shape[1:]
    rows = fine_rows // COARSEN
    cols = fine_cols // COARSEN
    sums[...] = dot(traj_ref[0].reshape(levels * fine_rows, fine_cols), pool_ref[...])
    total = sums[pl.ds(0, levels * rows, stride=COARSEN), :]
    for t in range(1, COARSEN):
        total = total + sums[pl.ds(t, levels * rows, stride=COARSEN), :]
    drift = advection_scale * jnp.tanh(total * (1.0 / (COARSEN * COARSEN)))
    drift = drift[:, :cols].reshape(levels, rows, cols)
    items = [back_ref[f] for f in range(FIELDS)] + [drift, weight_ref[...]]
    items += [depart_ref[f] for f in range(FIELDS)]
    for group in range(ITEMS // 4):
        out_ref[:, group] = jnp.concatenate(items[4 * group : 4 * group + 4], axis=-1)


def stencil(q, drift):
    rows, cycle = q.shape[-2:]
    north = pltpu.roll(q, 1, q.ndim - 2)
    south = pltpu.roll(q, rows - 1, q.ndim - 2)
    east = pltpu.roll(q, cycle - 1, q.ndim - 1)
    west = pltpu.roll(q, 1, q.ndim - 1)
    return q + diffusion * (north + south + east + west - 4.0 * q) + drift * (east - west)


def stencil_transposed(g, drift):
    rows, cycle = g.shape[-2:]
    north = pltpu.roll(g, 1, g.ndim - 2)
    south = pltpu.roll(g, rows - 1, g.ndim - 2)
    east = pltpu.roll(g, cycle - 1, g.ndim - 1)
    west = pltpu.roll(g, 1, g.ndim - 1)
    carried = drift * g
    return (
        g
        + diffusion * (north + south + east + west - 4.0 * g)
        + pltpu.roll(carried, 1, g.ndim - 1)
        - pltpu.roll(carried, cycle - 1, g.ndim - 1)
    )


def sweep_kernel(
    wide_count, narrow_count, levels, chunk,
    x_ref, response_ref, wave_high_ref, wave_low_ref, out_ref,
    landed, fields, result, outgoing, up_out, down_out, up_in, down_in,
    local_sem, send_sem, recv_sem, halo_send, halo_recv, back_send, back_recv,
):
    me = lax.axis_index("wide")
    band = lax.axis_index("narrow")
    has_above = band > 0
    has_below = band < narrow_count - 1
    rows = landed.shape[2]
    cycle = fields.shape[2]
    half = cycle // 2
    cols = cycle // wide_count
    padded = fields.shape[1]
    groups = out_ref.shape[1]

    barrier = pltpu.get_barrier_semaphore()
    for k in range(1, wide_count):
        pl.semaphore_signal(
            barrier, inc=1, device_id=(lax.rem(me + k, wide_count), band), device_id_type=MESH
        )

    @pl.when(has_above)
    def _():
        pl.semaphore_signal(barrier, inc=1, device_id=(me, band - 1), device_id_type=MESH)

    @pl.when(has_below)
    def _():
        pl.semaphore_signal(barrier, inc=1, device_id=(me, band + 1), device_id_type=MESH)

    keep = pltpu.make_async_copy(x_ref.at[me], landed.at[me], local_sem.at[0])
    keep.start()
    neighbours = has_above.astype(jnp.int32) + has_below.astype(jnp.int32)
    pl.semaphore_wait(barrier, wide_count - 1 + neighbours)

    turns = levels // chunk
    packed = chunk * (ITEMS // 4)
    sends = [[None] * wide_count for _ in range(turns)]
    for turn in range(turns):
        for k in range(1, wide_count):
            peer = lax.rem(me + k, wide_count)
            copy = pltpu.make_async_remote_copy(
                src_ref=x_ref.at[peer, pl.ds(turn * packed, packed)],
                dst_ref=landed.at[me, pl.ds(turn * packed, packed)],
                send_sem=send_sem.at[turn, k],
                recv_sem=recv_sem.at[turn, k],
                device_id=(peer, band),
                device_id_type=MESH,
            )
            copy.start()
            sends[turn][k] = copy

    low_half = lax.broadcasted_iota(jnp.int32, (8, half), 0) < HALO

    def unpack(level, carry):
        for group in range(ITEMS // 4):
            for tile in range(cycle // LANES):
                got = [landed[4 * tile + m, level * (ITEMS // 4) + group] for m in range(4)]
                for j, value in enumerate(block_transpose(got, cols)):
                    fields[level * ITEMS + 4 * group + j, 0:rows, tile * LANES : (tile + 1) * LANES] = value
        for item in range(ITEMS):
            at = level * ITEMS + item
            top = fields[at, 0:8]
            bottom = fields[at, rows - 8 : rows]
            up_out[at] = jnp.where(low_half, top[:, :half], pltpu.roll(top[:, half:], HALO, 0))
            down_out[at] = jnp.where(low_half, pltpu.roll(bottom[:, :half], HALO, 0), bottom[:, half:])
        return carry

    def halo_copies(turn):
        part = pl.ds(turn * chunk * ITEMS, chunk * ITEMS)
        up_copy = pltpu.make_async_remote_copy(
            src_ref=up_out.at[part], dst_ref=up_in.at[part],
            send_sem=halo_send.at[turn, 0], recv_sem=halo_recv.at[turn, 0],
            device_id=(me, band - 1), device_id_type=MESH,
        )
        down_copy = pltpu.make_async_remote_copy(
            src_ref=down_out.at[part], dst_ref=down_in.at[part],
            send_sem=halo_send.at[turn, 1], recv_sem=halo_recv.at[turn, 1],
            device_id=(me, band + 1), device_id_type=MESH,
        )
        return up_copy, down_copy

    @pl.when(jnp.logical_not(has_below))
    def _():
        up_in[...] = jnp.zeros_like(up_in)

    @pl.when(jnp.logical_not(has_above))
    def _():
        down_in[...] = jnp.zeros_like(down_in)

    def take_halo(level, carry):
        for item in range(ITEMS):
            at = level * ITEMS + item
            below, above = up_in[at], down_in[at]
            fields[at, rows:padded, 0:half] = jnp.where(low_half, below, pltpu.roll(above, HALO, 0))
            fields[at, rows:padded, half:cycle] = jnp.where(low_half, pltpu.roll(below, HALO, 0), above)
        return carry

    def zonal(q):
        shape = q.shape
        high, low = split_bf16(q.reshape(-1, cycle))
        wave_high, wave_low = wave_high_ref[...], wave_low_ref[...]
        spectrum = dot(high, wave_high) + dot(low, wave_high) + dot(high, wave_low)
        spectrum = spectrum.reshape(shape) * response_ref[...]
        high, low = split_bf16(spectrum.reshape(-1, cycle))
        return (dot(high, wave_high) + dot(low, wave_high) + dot(high, wave_low)).reshape(shape)

    def sweep(turn):
        at = turn * chunk
        block = fields[pl.ds(at * ITEMS, chunk * ITEMS)].reshape(chunk, ITEMS, padded, cycle)
        background = block[:, :FIELDS]
        drift = block[:, FIELDS : FIELDS + 1]
        weight = block[:, FIELDS + 1 : FIELDS + 2]
        departure = block[:, FIELDS + 2 :]
        state = background
        for _ in range(STEPS):
            state = zonal(stencil(state, drift))
        costate = weight * (state - departure)
        for _ in range(STEPS):
            costate = stencil_transposed(zonal(costate), drift)
        increment = background - descent_step * ((background - background) + costate)
        result[0 : chunk * FIELDS] = increment.reshape(chunk * FIELDS, padded, cycle)[:, :rows]

    each = groups // turns

    def send_back(turn):
        def repack(group, carry):
            for tile in range(cycle // LANES):
                parts = [result[4 * group + j, :, tile * LANES : (tile + 1) * LANES] for j in range(4)]
                for m, value in enumerate(block_transpose(parts, cols)):
                    outgoing[4 * tile + m, turn * each + group] = value
            return carry

        lax.fori_loop(0, each, repack, 0)
        part = pl.ds(turn * each, each)
        keep_back = pltpu.make_async_copy(
            outgoing.at[me, part], out_ref.at[me, part], back_send.at[turn, 0]
        )
        keep_back.start()
        backs = [keep_back]
        for k in range(1, wide_count):
            peer = lax.rem(me + k, wide_count)
            copy = pltpu.make_async_remote_copy(
                src_ref=outgoing.at[peer, part],
                dst_ref=out_ref.at[me, part],
                send_sem=back_send.at[turn, k],
                recv_sem=back_recv.at[turn, k],
                device_id=(peer, band),
                device_id_type=MESH,
            )
            copy.start()
            backs.append(copy)
        return backs

    def compute(turn):
        up_copy, down_copy = halo_copies(turn)

        @pl.when(has_below)
        def _():
            up_copy.wait_recv()

        @pl.when(has_above)
        def _():
            down_copy.wait_recv()

        lax.fori_loop(turn * chunk, (turn + 1) * chunk, take_halo, 0)
        sweep(turn)
        return send_back(turn)

    keep.wait()
    backs = []
    for turn in range(turns):
        for k in range(1, wide_count):
            sends[turn][k].wait_recv()
        lax.fori_loop(turn * chunk, (turn + 1) * chunk, unpack, 0)
        up_copy, down_copy = halo_copies(turn)

        @pl.when(has_above)
        def _():
            up_copy.start()

        @pl.when(has_below)
        def _():
            down_copy.start()

        if turn > 0:
            backs += compute(turn - 1)
    backs += compute(turns - 1)

    for turn in range(turns):
        for k in range(1, wide_count):
            sends[turn][k].wait_send()
        up_copy, down_copy = halo_copies(turn)

        @pl.when(has_above)
        def _():
            up_copy.wait_send()

        @pl.when(has_below)
        def _():
            down_copy.wait_send()

    for copy in backs:
        copy.wait()


def finish_kernel(chunk, traj_ref, inc_ref, spread_ref, out_ref, wide, tall):
    fields, levels, fine_rows, fine_cols = traj_ref.shape
    groups, rows = inc_ref.shape[1:3]
    high, low = split_bf16(inc_ref[0].reshape(groups * rows, LANES))
    wide[...] = dot(high, spread_ref[...]) + dot(low, spread_ref[...])
    for level in range(levels):
        for f in range(fields):
            item = level * fields + f
            turn, place = divmod(item, chunk * fields)
            group, j = turn * (groups // (levels // chunk)) + place // 4, place % 4
            part = wide[group * rows : (group + 1) * rows, j * LANES : (j + 1) * LANES]
            for t in range(COARSEN):
                tall[item, pl.ds(t, rows, stride=COARSEN), :] = part
            out_ref[f, level] = (traj_ref[f, level].astype(jnp.float32) + tall[item]).astype(jnp.bfloat16)


def shards(trajectory, innovation, background, obs_weight):
    wide_count = lax.axis_size("wide")
    narrow_count = lax.axis_size("narrow")
    narrow_index = lax.axis_index("narrow")
    fields, total_levels, rows, cols = innovation.shape
    fine_rows, fine_cols = trajectory.shape[2:]
    cycle = cols * wide_count
    total_rows = rows * narrow_count
    levels = -(-total_levels // wide_count)
    last = -(-total_levels // levels) - 1
    chunk = max(c for c in range(1, 6) if levels % c == 0)
    packed = ITEMS // 4
    turns = levels // chunk
    groups = turns * -(-fields * chunk // 4)
    padded = rows + 2 * HALO

    lane = np.arange(fine_cols)
    pool = np.zeros((fine_cols, LANES), np.float32)
    pool[lane, lane // COARSEN] = 1.0
    spread = np.zeros((LANES, 4 * LANES), np.float32)
    for j in range(4):
        spread[j * cols + lane // COARSEN, j * LANES + lane] = 1.0
    pool = jnp.asarray(pool, jnp.bfloat16)
    spread = jnp.asarray(spread, jnp.bfloat16)

    sent = pl.pallas_call(
        pack_kernel,
        grid=(wide_count,),
        in_specs=[
            pl.BlockSpec((1, levels, fine_rows, fine_cols), lambda s: (0, jnp.minimum(s, last), 0, 0)),
            pl.BlockSpec((fields, levels, rows, cols), lambda s: (0, jnp.minimum(s, last), 0, 0)),
            pl.BlockSpec((fields, levels, rows, cols), lambda s: (0, jnp.minimum(s, last), 0, 0)),
            pl.BlockSpec((levels, rows, cols), lambda s: (jnp.minimum(s, last), 0, 0)),
            pl.BlockSpec((fine_cols, LANES), lambda s: (0, 0)),
        ],
        out_specs=pl.BlockSpec((levels, packed, rows, LANES), lambda s: (s, 0, 0, 0)),
        out_shape=jax.ShapeDtypeStruct((wide_count * levels, packed, rows, LANES), jnp.float32),
        scratch_shapes=[pltpu.VMEM((levels * fine_rows, LANES), jnp.float32)],
        name="pack",
    )(trajectory, innovation, background, obs_weight, pool)
    sent = sent.reshape(wide_count, levels * packed, rows, LANES)

    place = jnp.arange(padded, dtype=jnp.int32)
    row_index = jnp.where(place < rows + HALO, place, place - padded) + narrow_index * rows
    wavenumber = jnp.arange(cycle, dtype=jnp.int32)
    folded = jnp.minimum(wavenumber, cycle - wavenumber).astype(jnp.float32)
    latitude = jnp.pi * ((row_index.astype(jnp.float32) + 0.5) / total_rows - 0.5)
    cutoff = 0.5 * cycle * jnp.cos(latitude)
    inside = (row_index >= 0) & (row_index < total_rows)
    cutoff = jnp.where(inside, cutoff, 1.0)
    response = 1.0 / (1.0 + (folded[None, :] / cutoff[:, None]) ** 4)
    response = jnp.where(inside[:, None], response, 0.0) / cycle

    phase = np.arange(cycle)[:, None] * np.arange(cycle)[None, :] % cycle
    wave = np.cos(2.0 * np.pi / cycle * phase) + np.sin(2.0 * np.pi / cycle * phase)
    wave = wave.astype(np.float32)
    wave_high = wave.astype(jnp.bfloat16)
    wave_low = (wave - wave_high.astype(np.float32)).astype(jnp.bfloat16)

    vmem = pl.BlockSpec(memory_space=pltpu.VMEM)
    anywhere = pl.BlockSpec(memory_space=pl.ANY)
    f32 = jnp.float32
    moved_back = pl.pallas_call(
        functools.partial(sweep_kernel, wide_count, narrow_count, levels, chunk),
        in_specs=[anywhere, vmem, vmem, vmem],
        out_specs=anywhere,
        out_shape=jax.ShapeDtypeStruct((wide_count, groups, rows, LANES), f32),
        scratch_shapes=[
            pltpu.VMEM((wide_count, levels * packed, rows, LANES), f32),
            pltpu.VMEM((levels * ITEMS, padded, cycle), f32),
            pltpu.VMEM((groups // turns * 4, rows, cycle), f32),
            pltpu.VMEM((wide_count, groups, rows, LANES), f32),
            pltpu.VMEM((levels * ITEMS, 8, cycle // 2), f32),
            pltpu.VMEM((levels * ITEMS, 8, cycle // 2), f32),
            pltpu.VMEM((levels * ITEMS, 8, cycle // 2), f32),
            pltpu.VMEM((levels * ITEMS, 8, cycle // 2), f32),
            pltpu.SemaphoreType.DMA((1,)),
            pltpu.SemaphoreType.DMA((turns, wide_count)),
            pltpu.SemaphoreType.DMA((turns, wide_count)),
            pltpu.SemaphoreType.DMA((turns, 2)),
            pltpu.SemaphoreType.DMA((turns, 2)),
            pltpu.SemaphoreType.DMA((turns, wide_count)),
            pltpu.SemaphoreType.DMA((turns, wide_count)),
        ],
        compiler_params=pltpu.CompilerParams(collective_id=0, has_side_effects=True),
        name="sweep",
    )(sent, response, jnp.asarray(wave_high), jnp.asarray(wave_low))

    return pl.pallas_call(
        functools.partial(finish_kernel, chunk),
        grid=(last + 1,),
        in_specs=[
            pl.BlockSpec((fields, levels, fine_rows, fine_cols), lambda s: (0, s, 0, 0)),
            pl.BlockSpec((1, groups, rows, LANES), lambda s: (s, 0, 0, 0)),
            pl.BlockSpec((LANES, 4 * LANES), lambda s: (0, 0)),
        ],
        out_specs=pl.BlockSpec((fields, levels, fine_rows, fine_cols), lambda s: (0, s, 0, 0)),
        out_shape=jax.ShapeDtypeStruct(trajectory.shape, jnp.bfloat16),
        scratch_shapes=[
            pltpu.VMEM((groups * rows, 4 * LANES), f32),
            pltpu.VMEM((fields * levels, fine_rows, fine_cols), f32),
        ],
        name="finish",
    )(trajectory, moved_back, spread)


def solution(mesh):
    in_specs = (
        P(None, None, "narrow", "wide"),
        P(None, None, "narrow", "wide"),
        P(None, None, "narrow", "wide"),
        P(None, "narrow", "wide"),
    )
    out_specs = P(None, None, "narrow", "wide")
    return jax.shard_map(shards, mesh=mesh, in_specs=in_specs, out_specs=out_specs, check_vma=False)
```

```python
import functools

import jax
import jax.numpy as jnp
import numpy as np
from jax import lax
from jax.experimental import pallas as pl
from jax.experimental.pallas import tpu as pltpu
from jax.sharding import PartitionSpec as P

MESH = pl.DeviceIdType.MESH
FIELDS = 5
COARSEN = 4
STEPS = 2
LANES = 128
HALO = 2 * STEPS
ITEMS = 2 * FIELDS + 2

diffusion = 0.2
advection_scale = 0.3
descent_step = 1.0


def split_bf16(x):
    high = x.astype(jnp.bfloat16)
    low = (x - high.astype(jnp.float32)).astype(jnp.bfloat16)
    return high, low


def dot(a, b):
    return jnp.dot(a, b, preferred_element_type=jnp.float32)


def block_transpose(tiles, block):
    lane = lax.broadcasted_iota(jnp.int32, tiles[0].shape, len(tiles[0].shape) - 1) // block
    axis = len(tiles[0].shape) - 1
    tiles = list(tiles)
    for step in (2, 1):
        upper = (lane // step) % 2 == 1
        for first in range(4):
            if (first // step) % 2 == 0:
                second = first + step
                a, b = tiles[first], tiles[second]
                tiles[first] = jnp.where(upper, pltpu.roll(b, step * block, axis), a)
                tiles[second] = jnp.where(upper, b, pltpu.roll(a, LANES - step * block, axis))
    return tiles


def pack_kernel(traj_ref, depart_ref, back_ref, weight_ref, pool_ref, out_ref, sums):
    levels, fine_rows, fine_cols = traj_ref.shape[1:]
    rows, cols = weight_ref.shape[:2]
    sums[...] = dot(traj_ref[0].reshape(levels * fine_rows, fine_cols), pool_ref[...])
    total = sums[pl.ds(0, levels * rows, stride=COARSEN), :]
    for t in range(1, COARSEN):
        total = total + sums[pl.ds(t, levels * rows, stride=COARSEN), :]
    drift = advection_scale * jnp.tanh(total * (1.0 / (COARSEN * COARSEN)))
    drift = drift.reshape(levels, rows, LANES)
    is_drift = lax.broadcasted_iota(jnp.int32, drift.shape, 2) // cols == 1

    def item(index, row):
        if index < FIELDS:
            return back_ref[index, row]
        if index < FIELDS + 2:
            return weight_ref[row]
        return depart_ref[index - FIELDS - 2, row]

    for group in range(ITEMS // 4):
        lines = []
        for row in range(rows):
            stacked = jnp.concatenate([item(4 * group + j, row) for j in range(4)], axis=0)
            lines.append(stacked.T)
        value = jnp.swapaxes(jnp.stack(lines), 0, 1)
        if group == FIELDS // 4:
            value = jnp.where(is_drift, drift, value)
        out_ref[:, group] = value


def stencil(q, drift):
    rows, cycle = q.shape[-2:]
    north = pltpu.roll(q, 1, q.ndim - 2)
    south = pltpu.roll(q, rows - 1, q.ndim - 2)
    east = pltpu.roll(q, cycle - 1, q.ndim - 1)
    west = pltpu.roll(q, 1, q.ndim - 1)
    return q + diffusion * (north + south + east + west - 4.0 * q) + drift * (east - west)


def stencil_transposed(g, drift):
    rows, cycle = g.shape[-2:]
    north = pltpu.roll(g, 1, g.ndim - 2)
    south = pltpu.roll(g, rows - 1, g.ndim - 2)
    east = pltpu.roll(g, cycle - 1, g.ndim - 1)
    west = pltpu.roll(g, 1, g.ndim - 1)
    carried = drift * g
    return (
        g
        + diffusion * (north + south + east + west - 4.0 * g)
        + pltpu.roll(carried, 1, g.ndim - 1)
        - pltpu.roll(carried, cycle - 1, g.ndim - 1)
    )


def sweep_kernel(
    wide_count, narrow_count, levels, chunk,
    x_ref, response_ref, wave_high_ref, wave_low_ref, out_ref,
    landed, fields, result, outgoing, up_out, down_out, up_in, down_in,
    local_sem, send_sem, recv_sem, halo_send, halo_recv, back_send, back_recv,
):
    me = lax.axis_index("wide")
    band = lax.axis_index("narrow")
    has_above = band > 0
    has_below = band < narrow_count - 1
    rows = landed.shape[2]
    cycle = fields.shape[2]
    half = cycle // 2
    cols = cycle // wide_count
    padded = fields.shape[1]
    groups = out_ref.shape[1]

    barrier = pltpu.get_barrier_semaphore()
    for k in range(1, wide_count):
        pl.semaphore_signal(
            barrier, inc=1, device_id=(lax.rem(me + k, wide_count), band), device_id_type=MESH
        )

    @pl.when(has_above)
    def _():
        pl.semaphore_signal(barrier, inc=1, device_id=(me, band - 1), device_id_type=MESH)

    @pl.when(has_below)
    def _():
        pl.semaphore_signal(barrier, inc=1, device_id=(me, band + 1), device_id_type=MESH)

    keep = pltpu.make_async_copy(x_ref.at[me], landed.at[me], local_sem.at[0])
    keep.start()
    neighbours = has_above.astype(jnp.int32) + has_below.astype(jnp.int32)
    pl.semaphore_wait(barrier, wide_count - 1 + neighbours)

    turns = levels // chunk
    packed = chunk * (ITEMS // 4)
    sends = [[None] * wide_count for _ in range(turns)]
    for turn in range(turns):
        for k in range(1, wide_count):
            peer = lax.rem(me + k, wide_count)
            copy = pltpu.make_async_remote_copy(
                src_ref=x_ref.at[peer, pl.ds(turn * packed, packed)],
                dst_ref=landed.at[me, pl.ds(turn * packed, packed)],
                send_sem=send_sem.at[turn, k],
                recv_sem=recv_sem.at[turn, k],
                device_id=(peer, band),
                device_id_type=MESH,
            )
            copy.start()
            sends[turn][k] = copy

    low_half = lax.broadcasted_iota(jnp.int32, (8, half), 0) < HALO

    def unpack(level, carry):
        for group in range(ITEMS // 4):
            for tile in range(cycle // LANES):
                got = [landed[4 * tile + m, level * (ITEMS // 4) + group] for m in range(4)]
                for j, value in enumerate(block_transpose(got, cols)):
                    fields[level * ITEMS + 4 * group + j, 0:rows, tile * LANES : (tile + 1) * LANES] = value
        for item in range(ITEMS):
            at = level * ITEMS + item
            top = fields[at, 0:8]
            bottom = fields[at, rows - 8 : rows]
            up_out[at] = jnp.where(low_half, top[:, :half], pltpu.roll(top[:, half:], HALO, 0))
            down_out[at] = jnp.where(low_half, pltpu.roll(bottom[:, :half], HALO, 0), bottom[:, half:])
        return carry

    def halo_copies(turn):
        part = pl.ds(turn * chunk * ITEMS, chunk * ITEMS)
        up_copy = pltpu.make_async_remote_copy(
            src_ref=up_out.at[part], dst_ref=up_in.at[part],
            send_sem=halo_send.at[turn, 0], recv_sem=halo_recv.at[turn, 0],
            device_id=(me, band - 1), device_id_type=MESH,
        )
        down_copy = pltpu.make_async_remote_copy(
            src_ref=down_out.at[part], dst_ref=down_in.at[part],
            send_sem=halo_send.at[turn, 1], recv_sem=halo_recv.at[turn, 1],
            device_id=(me, band + 1), device_id_type=MESH,
        )
        return up_copy, down_copy

    @pl.when(jnp.logical_not(has_below))
    def _():
        up_in[...] = jnp.zeros_like(up_in)

    @pl.when(jnp.logical_not(has_above))
    def _():
        down_in[...] = jnp.zeros_like(down_in)

    def take_halo(level, carry):
        for item in range(ITEMS):
            at = level * ITEMS + item
            below, above = up_in[at], down_in[at]
            fields[at, rows:padded, 0:half] = jnp.where(low_half, below, pltpu.roll(above, HALO, 0))
            fields[at, rows:padded, half:cycle] = jnp.where(low_half, pltpu.roll(below, HALO, 0), above)
        return carry

    def zonal(q):
        shape = q.shape
        high, low = split_bf16(q.reshape(-1, cycle))
        wave_high, wave_low = wave_high_ref[...], wave_low_ref[...]
        spectrum = dot(high, wave_high) + dot(low, wave_high) + dot(high, wave_low)
        spectrum = spectrum.reshape(shape) * response_ref[...]
        high, low = split_bf16(spectrum.reshape(-1, cycle))
        return (dot(high, wave_high) + dot(low, wave_high) + dot(high, wave_low)).reshape(shape)

    def sweep(turn):
        at = turn * chunk
        block = fields[pl.ds(at * ITEMS, chunk * ITEMS)].reshape(chunk, ITEMS, padded, cycle)
        background = block[:, :FIELDS]
        drift = block[:, FIELDS : FIELDS + 1]
        weight = block[:, FIELDS + 1 : FIELDS + 2]
        departure = block[:, FIELDS + 2 :]
        state = background
        for _ in range(STEPS):
            state = zonal(stencil(state, drift))
        costate = weight * (state - departure)
        for _ in range(STEPS):
            costate = stencil_transposed(zonal(costate), drift)
        increment = background - descent_step * ((background - background) + costate)
        result[0 : chunk * FIELDS] = increment.reshape(chunk * FIELDS, padded, cycle)[:, :rows]

    each = groups // turns

    def send_back(turn):
        def repack(group, carry):
            for tile in range(cycle // LANES):
                parts = [result[4 * group + j, :, tile * LANES : (tile + 1) * LANES] for j in range(4)]
                for m, value in enumerate(block_transpose(parts, cols)):
                    outgoing[4 * tile + m, turn * each + group] = value
            return carry

        lax.fori_loop(0, each, repack, 0)
        part = pl.ds(turn * each, each)
        keep_back = pltpu.make_async_copy(
            outgoing.at[me, part], out_ref.at[me, part], back_send.at[turn, 0]
        )
        keep_back.start()
        backs = [keep_back]
        for k in range(1, wide_count):
            peer = lax.rem(me + k, wide_count)
            copy = pltpu.make_async_remote_copy(
                src_ref=outgoing.at[peer, part],
                dst_ref=out_ref.at[me, part],
                send_sem=back_send.at[turn, k],
                recv_sem=back_recv.at[turn, k],
                device_id=(peer, band),
                device_id_type=MESH,
            )
            copy.start()
            backs.append(copy)
        return backs

    def compute(turn):
        up_copy, down_copy = halo_copies(turn)

        @pl.when(has_below)
        def _():
            up_copy.wait_recv()

        @pl.when(has_above)
        def _():
            down_copy.wait_recv()

        lax.fori_loop(turn * chunk, (turn + 1) * chunk, take_halo, 0)
        sweep(turn)
        return send_back(turn)

    keep.wait()
    backs = []
    for turn in range(turns):
        for k in range(1, wide_count):
            sends[turn][k].wait_recv()
        lax.fori_loop(turn * chunk, (turn + 1) * chunk, unpack, 0)
        up_copy, down_copy = halo_copies(turn)

        @pl.when(has_above)
        def _():
            up_copy.start()

        @pl.when(has_below)
        def _():
            down_copy.start()

        if turn > 0:
            backs += compute(turn - 1)
    backs += compute(turns - 1)

    for turn in range(turns):
        for k in range(1, wide_count):
            sends[turn][k].wait_send()
        up_copy, down_copy = halo_copies(turn)

        @pl.when(has_above)
        def _():
            up_copy.wait_send()

        @pl.when(has_below)
        def _():
            down_copy.wait_send()

    for copy in backs:
        copy.wait()


def finish_kernel(chunk, traj_ref, inc_ref, spread_ref, out_ref, wide, tall):
    fields, levels, fine_rows, fine_cols = traj_ref.shape
    groups, rows = inc_ref.shape[1:3]
    high, low = split_bf16(inc_ref[0].reshape(groups * rows, LANES))
    wide[...] = dot(high, spread_ref[...]) + dot(low, spread_ref[...])
    for level in range(levels):
        for f in range(fields):
            item = level * fields + f
            turn, place = divmod(item, chunk * fields)
            group, j = turn * (groups // (levels // chunk)) + place // 4, place % 4
            part = wide[group * rows : (group + 1) * rows, j * LANES : (j + 1) * LANES]
            for t in range(COARSEN):
                tall[item, pl.ds(t, rows, stride=COARSEN), :] = part
            out_ref[f, level] = (traj_ref[f, level].astype(jnp.float32) + tall[item]).astype(jnp.bfloat16)


def shards(trajectory, innovation, background, obs_weight):
    wide_count = lax.axis_size("wide")
    narrow_count = lax.axis_size("narrow")
    narrow_index = lax.axis_index("narrow")
    fields, total_levels, rows, cols = innovation.shape
    fine_rows, fine_cols = trajectory.shape[2:]
    cycle = cols * wide_count
    total_rows = rows * narrow_count
    levels = -(-total_levels // wide_count)
    last = -(-total_levels // levels) - 1
    chunk = max(c for c in range(1, 6) if levels % c == 0)
    packed = ITEMS // 4
    turns = levels // chunk
    groups = turns * -(-fields * chunk // 4)
    padded = rows + 2 * HALO

    lane = np.arange(fine_cols)
    pool = np.zeros((fine_cols, LANES), np.float32)
    pool[lane, FIELDS % 4 * cols + lane // COARSEN] = 1.0
    spread = np.zeros((LANES, 4 * LANES), np.float32)
    for j in range(4):
        spread[j * cols + lane // COARSEN, j * LANES + lane] = 1.0
    pool = jnp.asarray(pool, jnp.bfloat16)
    spread = jnp.asarray(spread, jnp.bfloat16)

    sent = pl.pallas_call(
        pack_kernel,
        grid=(rows // 8,),
        in_specs=[
            pl.BlockSpec((1, total_levels, 8 * COARSEN, fine_cols), lambda r: (0, 0, r, 0)),
            pl.BlockSpec((fields, 8, cols, total_levels), lambda r: (0, r, 0, 0)),
            pl.BlockSpec((fields, 8, cols, total_levels), lambda r: (0, r, 0, 0)),
            pl.BlockSpec((8, cols, total_levels), lambda r: (r, 0, 0)),
            pl.BlockSpec((fine_cols, LANES), lambda r: (0, 0)),
        ],
        out_specs=pl.BlockSpec((total_levels, packed, 8, LANES), lambda r: (0, 0, r, 0)),
        out_shape=jax.ShapeDtypeStruct((wide_count * levels, packed, rows, LANES), jnp.float32),
        scratch_shapes=[pltpu.VMEM((total_levels * 8 * COARSEN, LANES), jnp.float32)],
        name="pack",
    )(
        trajectory,
        innovation.transpose(0, 2, 3, 1),
        background.transpose(0, 2, 3, 1),
        obs_weight.transpose(1, 2, 0),
        pool,
    )
    sent = sent.reshape(wide_count, levels * packed, rows, LANES)

    place = jnp.arange(padded, dtype=jnp.int32)
    row_index = jnp.where(place < rows + HALO, place, place - padded) + narrow_index * rows
    wavenumber = jnp.arange(cycle, dtype=jnp.int32)
    folded = jnp.minimum(wavenumber, cycle - wavenumber).astype(jnp.float32)
    latitude = jnp.pi * ((row_index.astype(jnp.float32) + 0.5) / total_rows - 0.5)
    cutoff = 0.5 * cycle * jnp.cos(latitude)
    inside = (row_index >= 0) & (row_index < total_rows)
    cutoff = jnp.where(inside, cutoff, 1.0)
    response = 1.0 / (1.0 + (folded[None, :] / cutoff[:, None]) ** 4)
    response = jnp.where(inside[:, None], response, 0.0) / cycle

    phase = np.arange(cycle)[:, None] * np.arange(cycle)[None, :] % cycle
    wave = np.cos(2.0 * np.pi / cycle * phase) + np.sin(2.0 * np.pi / cycle * phase)
    wave = wave.astype(np.float32)
    wave_high = wave.astype(jnp.bfloat16)
    wave_low = (wave - wave_high.astype(np.float32)).astype(jnp.bfloat16)

    vmem = pl.BlockSpec(memory_space=pltpu.VMEM)
    anywhere = pl.BlockSpec(memory_space=pl.ANY)
    f32 = jnp.float32
    moved_back = pl.pallas_call(
        functools.partial(sweep_kernel, wide_count, narrow_count, levels, chunk),
        in_specs=[anywhere, vmem, vmem, vmem],
        out_specs=anywhere,
        out_shape=jax.ShapeDtypeStruct((wide_count, groups, rows, LANES), f32),
        scratch_shapes=[
            pltpu.VMEM((wide_count, levels * packed, rows, LANES), f32),
            pltpu.VMEM((levels * ITEMS, padded, cycle), f32),
            pltpu.VMEM((groups // turns * 4, rows, cycle), f32),
            pltpu.VMEM((wide_count, groups, rows, LANES), f32),
            pltpu.VMEM((levels * ITEMS, 8, cycle // 2), f32),
            pltpu.VMEM((levels * ITEMS, 8, cycle // 2), f32),
            pltpu.VMEM((levels * ITEMS, 8, cycle // 2), f32),
            pltpu.VMEM((levels * ITEMS, 8, cycle // 2), f32),
            pltpu.SemaphoreType.DMA((1,)),
            pltpu.SemaphoreType.DMA((turns, wide_count)),
            pltpu.SemaphoreType.DMA((turns, wide_count)),
            pltpu.SemaphoreType.DMA((turns, 2)),
            pltpu.SemaphoreType.DMA((turns, 2)),
            pltpu.SemaphoreType.DMA((turns, wide_count)),
            pltpu.SemaphoreType.DMA((turns, wide_count)),
        ],
        compiler_params=pltpu.CompilerParams(collective_id=0, has_side_effects=True),
        name="sweep",
    )(sent, response, jnp.asarray(wave_high), jnp.asarray(wave_low))

    return pl.pallas_call(
        functools.partial(finish_kernel, chunk),
        grid=(last + 1,),
        in_specs=[
            pl.BlockSpec((fields, levels, fine_rows, fine_cols), lambda s: (0, s, 0, 0)),
            pl.BlockSpec((1, groups, rows, LANES), lambda s: (s, 0, 0, 0)),
            pl.BlockSpec((LANES, 4 * LANES), lambda s: (0, 0)),
        ],
        out_specs=pl.BlockSpec((fields, levels, fine_rows, fine_cols), lambda s: (0, s, 0, 0)),
        out_shape=jax.ShapeDtypeStruct(trajectory.shape, jnp.bfloat16),
        scratch_shapes=[
            pltpu.VMEM((groups * rows, 4 * LANES), f32),
            pltpu.VMEM((fields * levels, fine_rows, fine_cols), f32),
        ],
        name="finish",
    )(trajectory, moved_back, spread)


def solution(mesh):
    in_specs = (
        P(None, None, "narrow", "wide"),
        P(None, None, "narrow", "wide"),
        P(None, None, "narrow", "wide"),
        P(None, "narrow", "wide"),
    )
    out_specs = P(None, None, "narrow", "wide")
    return jax.shard_map(shards, mesh=mesh, in_specs=in_specs, out_specs=out_specs, check_vma=False)
```

```python
import functools

import jax
import jax.numpy as jnp
import numpy as np
from jax import lax
from jax.experimental import pallas as pl
from jax.experimental.pallas import tpu as pltpu
from jax.sharding import PartitionSpec as P

MESH = pl.DeviceIdType.MESH
FIELDS = 5
COARSEN = 4
STEPS = 2
LANES = 128
HALO = 2 * STEPS
ITEMS = 2 * FIELDS + 2

diffusion = 0.2
advection_scale = 0.3
descent_step = 1.0


def split_bf16(x):
    high = x.astype(jnp.bfloat16)
    low = (x - high.astype(jnp.float32)).astype(jnp.bfloat16)
    return high, low


def dot(a, b):
    return jnp.dot(a, b, preferred_element_type=jnp.float32)


def block_transpose(tiles, block):
    lane = lax.broadcasted_iota(jnp.int32, tiles[0].shape, len(tiles[0].shape) - 1) // block
    axis = len(tiles[0].shape) - 1
    tiles = list(tiles)
    for step in (2, 1):
        upper = (lane // step) % 2 == 1
        for first in range(4):
            if (first // step) % 2 == 0:
                second = first + step
                a, b = tiles[first], tiles[second]
                tiles[first] = jnp.where(upper, pltpu.roll(b, step * block, axis), a)
                tiles[second] = jnp.where(upper, b, pltpu.roll(a, LANES - step * block, axis))
    return tiles


def pack_kernel(traj_ref, depart_ref, back_ref, weight_ref, pool_ref, out_ref, sums):
    levels, fine_rows, fine_cols = traj_ref.shape[1:]
    rows, cols = weight_ref.shape[:2]
    sums[...] = dot(traj_ref[0].reshape(levels * fine_rows, fine_cols), pool_ref[...])
    total = sums[pl.ds(0, levels * rows, stride=COARSEN), :]
    for t in range(1, COARSEN):
        total = total + sums[pl.ds(t, levels * rows, stride=COARSEN), :]
    drift = advection_scale * jnp.tanh(total * (1.0 / (COARSEN * COARSEN)))
    drift = drift.reshape(levels, rows, LANES)
    is_drift = lax.broadcasted_iota(jnp.int32, drift.shape, 2) // cols == 1

    def item(index, row):
        if index < FIELDS:
            return back_ref[index, row]
        if index < FIELDS + 2:
            return weight_ref[row]
        return depart_ref[index - FIELDS - 2, row]

    for group in range(ITEMS // 4):
        lines = []
        for row in range(rows):
            stacked = jnp.concatenate([item(4 * group + j, row) for j in range(4)], axis=0)
            lines.append(stacked.T)
        value = jnp.swapaxes(jnp.stack(lines), 0, 1)
        if group == FIELDS // 4:
            value = jnp.where(is_drift, drift, value)
        out_ref[:, group] = value


def stencil(q, drift):
    rows, cycle = q.shape[-2:]
    north = pltpu.roll(q, 1, q.ndim - 2)
    south = pltpu.roll(q, rows - 1, q.ndim - 2)
    east = pltpu.roll(q, cycle - 1, q.ndim - 1)
    west = pltpu.roll(q, 1, q.ndim - 1)
    return q + diffusion * (north + south + east + west - 4.0 * q) + drift * (east - west)


def stencil_transposed(g, drift):
    rows, cycle = g.shape[-2:]
    north = pltpu.roll(g, 1, g.ndim - 2)
    south = pltpu.roll(g, rows - 1, g.ndim - 2)
    east = pltpu.roll(g, cycle - 1, g.ndim - 1)
    west = pltpu.roll(g, 1, g.ndim - 1)
    carried = drift * g
    return (
        g
        + diffusion * (north + south + east + west - 4.0 * g)
        + pltpu.roll(carried, 1, g.ndim - 1)
        - pltpu.roll(carried, cycle - 1, g.ndim - 1)
    )


def sweep_kernel(
    wide_count, narrow_count, levels, chunk,
    x_ref, response_ref, wave_high_ref, wave_low_ref, out_ref,
    landed, fields, result, outgoing, up_out, down_out, up_in, down_in,
    local_sem, send_sem, recv_sem, halo_send, halo_recv, back_send, back_recv,
):
    me = lax.axis_index("wide")
    band = lax.axis_index("narrow")
    has_above = band > 0
    has_below = band < narrow_count - 1
    rows = landed.shape[2]
    cycle = fields.shape[2]
    half = cycle // 2
    cols = cycle // wide_count
    padded = fields.shape[1]
    groups = out_ref.shape[1]

    barrier = pltpu.get_barrier_semaphore()
    for k in range(1, wide_count):
        pl.semaphore_signal(
            barrier, inc=1, device_id=(lax.rem(me + k, wide_count), band), device_id_type=MESH
        )

    @pl.when(has_above)
    def _():
        pl.semaphore_signal(barrier, inc=1, device_id=(me, band - 1), device_id_type=MESH)

    @pl.when(has_below)
    def _():
        pl.semaphore_signal(barrier, inc=1, device_id=(me, band + 1), device_id_type=MESH)

    keep = pltpu.make_async_copy(x_ref.at[me], landed.at[me], local_sem.at[0])
    keep.start()
    neighbours = has_above.astype(jnp.int32) + has_below.astype(jnp.int32)
    pl.semaphore_wait(barrier, wide_count - 1 + neighbours)

    turns = levels // chunk
    packed = chunk * (ITEMS // 4)
    sends = [[None] * wide_count for _ in range(turns)]
    for turn in range(turns):
        for k in range(1, wide_count):
            peer = lax.rem(me + k, wide_count)
            copy = pltpu.make_async_remote_copy(
                src_ref=x_ref.at[peer, pl.ds(turn * packed, packed)],
                dst_ref=landed.at[me, pl.ds(turn * packed, packed)],
                send_sem=send_sem.at[turn, k],
                recv_sem=recv_sem.at[turn, k],
                device_id=(peer, band),
                device_id_type=MESH,
            )
            copy.start()
            sends[turn][k] = copy

    low_half = lax.broadcasted_iota(jnp.int32, (8, half), 0) < HALO

    def unpack(level, carry):
        for group in range(ITEMS // 4):
            for tile in range(cycle // LANES):
                got = [landed[4 * tile + m, level * (ITEMS // 4) + group] for m in range(4)]
                for j, value in enumerate(block_transpose(got, cols)):
                    fields[level * ITEMS + 4 * group + j, 0:rows, tile * LANES : (tile + 1) * LANES] = value
        for item in range(ITEMS):
            at = level * ITEMS + item
            top = fields[at, 0:8]
            bottom = fields[at, rows - 8 : rows]
            up_out[at] = jnp.where(low_half, top[:, :half], pltpu.roll(top[:, half:], HALO, 0))
            down_out[at] = jnp.where(low_half, pltpu.roll(bottom[:, :half], HALO, 0), bottom[:, half:])
        return carry

    def halo_copies(turn):
        part = pl.ds(turn * chunk * ITEMS, chunk * ITEMS)
        up_copy = pltpu.make_async_remote_copy(
            src_ref=up_out.at[part], dst_ref=up_in.at[part],
            send_sem=halo_send.at[turn, 0], recv_sem=halo_recv.at[turn, 0],
            device_id=(me, band - 1), device_id_type=MESH,
        )
        down_copy = pltpu.make_async_remote_copy(
            src_ref=down_out.at[part], dst_ref=down_in.at[part],
            send_sem=halo_send.at[turn, 1], recv_sem=halo_recv.at[turn, 1],
            device_id=(me, band + 1), device_id_type=MESH,
        )
        return up_copy, down_copy

    @pl.when(jnp.logical_not(has_below))
    def _():
        up_in[...] = jnp.zeros_like(up_in)

    @pl.when(jnp.logical_not(has_above))
    def _():
        down_in[...] = jnp.zeros_like(down_in)

    def take_halo(level, carry):
        for item in range(ITEMS):
            at = level * ITEMS + item
            below, above = up_in[at], down_in[at]
            fields[at, rows:padded, 0:half] = jnp.where(low_half, below, pltpu.roll(above, HALO, 0))
            fields[at, rows:padded, half:cycle] = jnp.where(low_half, pltpu.roll(below, HALO, 0), above)
        return carry

    def zonal(q):
        shape = q.shape
        high, low = split_bf16(q.reshape(-1, cycle))
        wave_high, wave_low = wave_high_ref[...], wave_low_ref[...]
        spectrum = dot(high, wave_high) + dot(low, wave_high) + dot(high, wave_low)
        spectrum = spectrum.reshape(shape) * response_ref[...]
        high, low = split_bf16(spectrum.reshape(-1, cycle))
        return (dot(high, wave_high) + dot(low, wave_high) + dot(high, wave_low)).reshape(shape)

    def sweep(turn):
        at = turn * chunk
        block = fields[pl.ds(at * ITEMS, chunk * ITEMS)].reshape(chunk, ITEMS, padded, cycle)
        background = block[:, :FIELDS]
        drift = block[:, FIELDS : FIELDS + 1]
        weight = block[:, FIELDS + 1 : FIELDS + 2]
        departure = block[:, FIELDS + 2 :]
        state = background
        for _ in range(STEPS):
            state = zonal(stencil(state, drift))
        costate = weight * (state - departure)
        for _ in range(STEPS):
            costate = stencil_transposed(zonal(costate), drift)
        increment = background - descent_step * ((background - background) + costate)
        result[0 : chunk * FIELDS] = increment.reshape(chunk * FIELDS, padded, cycle)[:, :rows]

    each = groups // turns

    def send_back(turn):
        def repack(group, carry):
            for tile in range(cycle // LANES):
                parts = [result[4 * group + j, :, tile * LANES : (tile + 1) * LANES] for j in range(4)]
                for m, value in enumerate(block_transpose(parts, cols)):
                    outgoing[4 * tile + m, turn * each + group] = value
            return carry

        lax.fori_loop(0, each, repack, 0)
        part = pl.ds(turn * each, each)
        keep_back = pltpu.make_async_copy(
            outgoing.at[me, part], out_ref.at[me, part], back_send.at[turn, 0]
        )
        keep_back.start()
        backs = [keep_back]
        for k in range(1, wide_count):
            peer = lax.rem(me + k, wide_count)
            copy = pltpu.make_async_remote_copy(
                src_ref=outgoing.at[peer, part],
                dst_ref=out_ref.at[me, part],
                send_sem=back_send.at[turn, k],
                recv_sem=back_recv.at[turn, k],
                device_id=(peer, band),
                device_id_type=MESH,
            )
            copy.start()
            backs.append(copy)
        return backs

    def compute(turn):
        up_copy, down_copy = halo_copies(turn)

        @pl.when(has_below)
        def _():
            up_copy.wait_recv()

        @pl.when(has_above)
        def _():
            down_copy.wait_recv()

        lax.fori_loop(turn * chunk, (turn + 1) * chunk, take_halo, 0)
        sweep(turn)
        return send_back(turn)

    keep.wait()
    backs = []
    for turn in range(turns):
        for k in range(1, wide_count):
            sends[turn][k].wait_recv()
        lax.fori_loop(turn * chunk, (turn + 1) * chunk, unpack, 0)
        up_copy, down_copy = halo_copies(turn)

        @pl.when(has_above)
        def _():
            up_copy.start()

        @pl.when(has_below)
        def _():
            down_copy.start()

        if turn > 0:
            backs += compute(turn - 1)
    backs += compute(turns - 1)

    for turn in range(turns):
        for k in range(1, wide_count):
            sends[turn][k].wait_send()
        up_copy, down_copy = halo_copies(turn)

        @pl.when(has_above)
        def _():
            up_copy.wait_send()

        @pl.when(has_below)
        def _():
            down_copy.wait_send()

    for copy in backs:
        copy.wait()


def finish_kernel(chunk, traj_ref, inc_ref, spread_ref, out_ref, tall):
    fields, levels, fine_rows, fine_cols = traj_ref.shape
    groups, rows = inc_ref.shape[1:3]
    part = inc_ref[0].reshape(groups * rows, LANES)
    for t in range(COARSEN):
        tall[pl.ds(t, groups * rows, stride=COARSEN), :] = part
    each = groups // (levels // chunk)
    for turn in range(levels // chunk):
        span = each * fine_rows
        operand = jnp.concatenate(split_bf16(tall[turn * span : (turn + 1) * span]), axis=1)
        wide = dot(operand, spread_ref[...])
        for place in range(chunk * fields):
            level, f = divmod(turn * chunk * fields + place, fields)
            group, j = divmod(place, 4)
            fine = wide[group * fine_rows : (group + 1) * fine_rows, j * LANES : (j + 1) * LANES]
            out_ref[f, level] = (traj_ref[f, level].astype(jnp.float32) + fine).astype(jnp.bfloat16)


def shards(trajectory, innovation, background, obs_weight):
    wide_count = lax.axis_size("wide")
    narrow_count = lax.axis_size("narrow")
    narrow_index = lax.axis_index("narrow")
    fields, total_levels, rows, cols = innovation.shape
    fine_rows, fine_cols = trajectory.shape[2:]
    cycle = cols * wide_count
    total_rows = rows * narrow_count
    levels = -(-total_levels // wide_count)
    last = -(-total_levels // levels) - 1
    chunk = max(c for c in range(1, 6) if levels % c == 0)
    packed = ITEMS // 4
    turns = levels // chunk
    groups = turns * -(-fields * chunk // 4)
    padded = rows + 2 * HALO

    lane = np.arange(fine_cols)
    pool = np.zeros((fine_cols, LANES), np.float32)
    pool[lane, FIELDS % 4 * cols + lane // COARSEN] = 1.0
    spread = np.zeros((LANES, 4 * LANES), np.float32)
    for j in range(4):
        spread[j * cols + lane // COARSEN, j * LANES + lane] = 1.0
    pool = jnp.asarray(pool, jnp.bfloat16)
    spread = jnp.asarray(np.concatenate([spread, spread]), jnp.bfloat16)

    sent = pl.pallas_call(
        pack_kernel,
        grid=(rows // 8,),
        in_specs=[
            pl.BlockSpec((1, total_levels, 8 * COARSEN, fine_cols), lambda r: (0, 0, r, 0)),
            pl.BlockSpec((fields, 8, cols, total_levels), lambda r: (0, r, 0, 0)),
            pl.BlockSpec((fields, 8, cols, total_levels), lambda r: (0, r, 0, 0)),
            pl.BlockSpec((8, cols, total_levels), lambda r: (r, 0, 0)),
            pl.BlockSpec((fine_cols, LANES), lambda r: (0, 0)),
        ],
        out_specs=pl.BlockSpec((total_levels, packed, 8, LANES), lambda r: (0, 0, r, 0)),
        out_shape=jax.ShapeDtypeStruct((wide_count * levels, packed, rows, LANES), jnp.float32),
        scratch_shapes=[pltpu.VMEM((total_levels * 8 * COARSEN, LANES), jnp.float32)],
        name="pack",
    )(
        trajectory,
        innovation.transpose(0, 2, 3, 1),
        background.transpose(0, 2, 3, 1),
        obs_weight.transpose(1, 2, 0),
        pool,
    )
    sent = sent.reshape(wide_count, levels * packed, rows, LANES)

    place = jnp.arange(padded, dtype=jnp.int32)
    row_index = jnp.where(place < rows + HALO, place, place - padded) + narrow_index * rows
    wavenumber = jnp.arange(cycle, dtype=jnp.int32)
    folded = jnp.minimum(wavenumber, cycle - wavenumber).astype(jnp.float32)
    latitude = jnp.pi * ((row_index.astype(jnp.float32) + 0.5) / total_rows - 0.5)
    cutoff = 0.5 * cycle * jnp.cos(latitude)
    inside = (row_index >= 0) & (row_index < total_rows)
    cutoff = jnp.where(inside, cutoff, 1.0)
    response = 1.0 / (1.0 + (folded[None, :] / cutoff[:, None]) ** 4)
    response = jnp.where(inside[:, None], response, 0.0) / cycle

    phase = np.arange(cycle)[:, None] * np.arange(cycle)[None, :] % cycle
    wave = np.cos(2.0 * np.pi / cycle * phase) + np.sin(2.0 * np.pi / cycle * phase)
    wave = wave.astype(np.float32)
    wave_high = wave.astype(jnp.bfloat16)
    wave_low = (wave - wave_high.astype(np.float32)).astype(jnp.bfloat16)

    vmem = pl.BlockSpec(memory_space=pltpu.VMEM)
    anywhere = pl.BlockSpec(memory_space=pl.ANY)
    f32 = jnp.float32
    moved_back = pl.pallas_call(
        functools.partial(sweep_kernel, wide_count, narrow_count, levels, chunk),
        in_specs=[anywhere, vmem, vmem, vmem],
        out_specs=anywhere,
        out_shape=jax.ShapeDtypeStruct((wide_count, groups, rows, LANES), f32),
        scratch_shapes=[
            pltpu.VMEM((wide_count, levels * packed, rows, LANES), f32),
            pltpu.VMEM((levels * ITEMS, padded, cycle), f32),
            pltpu.VMEM((groups // turns * 4, rows, cycle), f32),
            pltpu.VMEM((wide_count, groups, rows, LANES), f32),
            pltpu.VMEM((levels * ITEMS, 8, cycle // 2), f32),
            pltpu.VMEM((levels * ITEMS, 8, cycle // 2), f32),
            pltpu.VMEM((levels * ITEMS, 8, cycle // 2), f32),
            pltpu.VMEM((levels * ITEMS, 8, cycle // 2), f32),
            pltpu.SemaphoreType.DMA((1,)),
            pltpu.SemaphoreType.DMA((turns, wide_count)),
            pltpu.SemaphoreType.DMA((turns, wide_count)),
            pltpu.SemaphoreType.DMA((turns, 2)),
            pltpu.SemaphoreType.DMA((turns, 2)),
            pltpu.SemaphoreType.DMA((turns, wide_count)),
            pltpu.SemaphoreType.DMA((turns, wide_count)),
        ],
        compiler_params=pltpu.CompilerParams(collective_id=0, has_side_effects=True),
        name="sweep",
    )(sent, response, jnp.asarray(wave_high), jnp.asarray(wave_low))

    return pl.pallas_call(
        functools.partial(finish_kernel, chunk),
        grid=(last + 1,),
        in_specs=[
            pl.BlockSpec((fields, levels, fine_rows, fine_cols), lambda s: (0, s, 0, 0)),
            pl.BlockSpec((1, groups, rows, LANES), lambda s: (s, 0, 0, 0)),
            pl.BlockSpec((2 * LANES, 4 * LANES), lambda s: (0, 0)),
        ],
        out_specs=pl.BlockSpec((fields, levels, fine_rows, fine_cols), lambda s: (0, s, 0, 0)),
        out_shape=jax.ShapeDtypeStruct(trajectory.shape, jnp.bfloat16),
        scratch_shapes=[
            pltpu.VMEM((groups * fine_rows, LANES), f32),
        ],
        name="finish",
    )(trajectory, moved_back, spread)


def solution(mesh):
    in_specs = (
        P(None, None, "narrow", "wide"),
        P(None, None, "narrow", "wide"),
        P(None, None, "narrow", "wide"),
        P(None, "narrow", "wide"),
    )
    out_specs = P(None, None, "narrow", "wide")
    return jax.shard_map(shards, mesh=mesh, in_specs=in_specs, out_specs=out_specs, check_vma=False)
```

```python
import functools

import jax
import jax.numpy as jnp
import numpy as np
from jax import lax
from jax.experimental import pallas as pl
from jax.experimental.pallas import tpu as pltpu
from jax.sharding import PartitionSpec as P

MESH = pl.DeviceIdType.MESH
FIELDS = 5
COARSEN = 4
STEPS = 2
LANES = 128
HALO = 2 * STEPS
ITEMS = 2 * FIELDS + 2

diffusion = 0.2
advection_scale = 0.3
descent_step = 1.0


def split_bf16(x):
    high = x.astype(jnp.bfloat16)
    low = (x - high.astype(jnp.float32)).astype(jnp.bfloat16)
    return high, low


def dot(a, b):
    return jnp.dot(a, b, preferred_element_type=jnp.float32)


def block_transpose(tiles, block):
    lane = lax.broadcasted_iota(jnp.int32, tiles[0].shape, len(tiles[0].shape) - 1) // block
    axis = len(tiles[0].shape) - 1
    tiles = list(tiles)
    for step in (2, 1):
        upper = (lane // step) % 2 == 1
        for first in range(4):
            if (first // step) % 2 == 0:
                second = first + step
                a, b = tiles[first], tiles[second]
                tiles[first] = jnp.where(upper, pltpu.roll(b, step * block, axis), a)
                tiles[second] = jnp.where(upper, b, pltpu.roll(a, LANES - step * block, axis))
    return tiles


def pack_kernel(traj_ref, depart_ref, back_ref, weight_ref, pool_ref, out_ref, sums):
    levels, fine_rows, fine_cols = traj_ref.shape[1:]
    rows, cols = weight_ref.shape[:2]
    sums[...] = dot(traj_ref[0].reshape(levels * fine_rows, fine_cols), pool_ref[...])
    total = sums[pl.ds(0, levels * rows, stride=COARSEN), :]
    for t in range(1, COARSEN):
        total = total + sums[pl.ds(t, levels * rows, stride=COARSEN), :]
    drift = advection_scale * jnp.tanh(total * (1.0 / (COARSEN * COARSEN)))
    drift = drift.reshape(levels, rows, LANES)
    is_drift = lax.broadcasted_iota(jnp.int32, drift.shape, 2) // cols == 1

    def item(index, row):
        if index < FIELDS:
            return back_ref[index, row]
        if index < FIELDS + 2:
            return weight_ref[row]
        return depart_ref[index - FIELDS - 2, row]

    for group in range(ITEMS // 4):
        lines = []
        for row in range(rows):
            stacked = jnp.concatenate([item(4 * group + j, row) for j in range(4)], axis=0)
            lines.append(stacked.T)
        value = jnp.swapaxes(jnp.stack(lines), 0, 1)
        if group == FIELDS // 4:
            value = jnp.where(is_drift, drift, value)
        out_ref[:, group] = value


def stencil(q, drift):
    rows, cycle = q.shape[-2:]
    north = pltpu.roll(q, 1, q.ndim - 2)
    south = pltpu.roll(q, rows - 1, q.ndim - 2)
    east = pltpu.roll(q, cycle - 1, q.ndim - 1)
    west = pltpu.roll(q, 1, q.ndim - 1)
    return q + diffusion * (north + south + east + west - 4.0 * q) + drift * (east - west)


def stencil_transposed(g, drift):
    rows, cycle = g.shape[-2:]
    north = pltpu.roll(g, 1, g.ndim - 2)
    south = pltpu.roll(g, rows - 1, g.ndim - 2)
    east = pltpu.roll(g, cycle - 1, g.ndim - 1)
    west = pltpu.roll(g, 1, g.ndim - 1)
    carried = drift * g
    return (
        g
        + diffusion * (north + south + east + west - 4.0 * g)
        + pltpu.roll(carried, 1, g.ndim - 1)
        - pltpu.roll(carried, cycle - 1, g.ndim - 1)
    )


def sweep_kernel(
    wide_count, narrow_count, levels, chunk,
    x_ref, response_ref, wave_high_ref, wave_low_ref, out_ref,
    landed, fields, result, outgoing, up_out, down_out, up_in, down_in,
    local_sem, send_sem, recv_sem, halo_send, halo_recv, back_send, back_recv,
):
    me = lax.axis_index("wide")
    band = lax.axis_index("narrow")
    has_above = band > 0
    has_below = band < narrow_count - 1
    rows = landed.shape[2]
    cycle = fields.shape[2]
    half = cycle // 2
    cols = cycle // wide_count
    padded = fields.shape[1]
    groups = out_ref.shape[1]

    barrier = pltpu.get_barrier_semaphore()
    for k in range(1, wide_count):
        pl.semaphore_signal(
            barrier, inc=1, device_id=(lax.rem(me + k, wide_count), band), device_id_type=MESH
        )

    @pl.when(has_above)
    def _():
        pl.semaphore_signal(barrier, inc=1, device_id=(me, band - 1), device_id_type=MESH)

    @pl.when(has_below)
    def _():
        pl.semaphore_signal(barrier, inc=1, device_id=(me, band + 1), device_id_type=MESH)

    keep = pltpu.make_async_copy(x_ref.at[me], landed.at[me], local_sem.at[0])
    keep.start()
    neighbours = has_above.astype(jnp.int32) + has_below.astype(jnp.int32)
    pl.semaphore_wait(barrier, wide_count - 1 + neighbours)

    turns = levels // chunk
    packed = chunk * (ITEMS // 4)
    sends = [[None] * wide_count for _ in range(turns)]
    for turn in range(turns):
        for k in range(1, wide_count):
            peer = lax.rem(me + k, wide_count)
            copy = pltpu.make_async_remote_copy(
                src_ref=x_ref.at[peer, pl.ds(turn * packed, packed)],
                dst_ref=landed.at[me, pl.ds(turn * packed, packed)],
                send_sem=send_sem.at[turn, k],
                recv_sem=recv_sem.at[turn, k],
                device_id=(peer, band),
                device_id_type=MESH,
            )
            copy.start()
            sends[turn][k] = copy

    low_half = lax.broadcasted_iota(jnp.int32, (8, half), 0) < HALO

    def unpack(level, carry):
        for group in range(ITEMS // 4):
            for tile in range(cycle // LANES):
                got = [landed[4 * tile + m, level * (ITEMS // 4) + group] for m in range(4)]
                for j, value in enumerate(block_transpose(got, cols)):
                    fields[level * ITEMS + 4 * group + j, 0:rows, tile * LANES : (tile + 1) * LANES] = value
        for item in range(ITEMS):
            at = level * ITEMS + item
            top = fields[at, 0:8]
            bottom = fields[at, rows - 8 : rows]
            up_out[at] = jnp.where(low_half, top[:, :half], pltpu.roll(top[:, half:], HALO, 0))
            down_out[at] = jnp.where(low_half, pltpu.roll(bottom[:, :half], HALO, 0), bottom[:, half:])
        return carry

    def halo_copies(turn):
        part = pl.ds(turn * chunk * ITEMS, chunk * ITEMS)
        up_copy = pltpu.make_async_remote_copy(
            src_ref=up_out.at[part], dst_ref=up_in.at[part],
            send_sem=halo_send.at[turn, 0], recv_sem=halo_recv.at[turn, 0],
            device_id=(me, band - 1), device_id_type=MESH,
        )
        down_copy = pltpu.make_async_remote_copy(
            src_ref=down_out.at[part], dst_ref=down_in.at[part],
            send_sem=halo_send.at[turn, 1], recv_sem=halo_recv.at[turn, 1],
            device_id=(me, band + 1), device_id_type=MESH,
        )
        return up_copy, down_copy

    @pl.when(jnp.logical_not(has_below))
    def _():
        up_in[...] = jnp.zeros_like(up_in)

    @pl.when(jnp.logical_not(has_above))
    def _():
        down_in[...] = jnp.zeros_like(down_in)

    def take_halo(level, carry):
        for item in range(ITEMS):
            at = level * ITEMS + item
            below, above = up_in[at], down_in[at]
            fields[at, rows:padded, 0:half] = jnp.where(low_half, below, pltpu.roll(above, HALO, 0))
            fields[at, rows:padded, half:cycle] = jnp.where(low_half, pltpu.roll(below, HALO, 0), above)
        return carry

    def zonal(q):
        shape = q.shape
        high, low = split_bf16(q.reshape(-1, cycle))
        wave_high, wave_low = wave_high_ref[...], wave_low_ref[...]
        spectrum = dot(high, wave_high) + dot(low, wave_high) + dot(high, wave_low)
        spectrum = spectrum.reshape(shape) * response_ref[...]
        high, low = split_bf16(spectrum.reshape(-1, cycle))
        return (dot(high, wave_high) + dot(low, wave_high) + dot(high, wave_low)).reshape(shape)

    def sweep(turn):
        at = turn * chunk
        block = fields[pl.ds(at * ITEMS, chunk * ITEMS)].reshape(chunk, ITEMS, padded, cycle)
        background = block[:, :FIELDS]
        drift = block[:, FIELDS : FIELDS + 1]
        weight = block[:, FIELDS + 1 : FIELDS + 2]
        departure = block[:, FIELDS + 2 :]
        state = background
        for _ in range(STEPS):
            state = zonal(stencil(state, drift))
        costate = weight * (state - departure)
        for _ in range(STEPS):
            costate = stencil_transposed(zonal(costate), drift)
        increment = background - descent_step * ((background - background) + costate)
        result[0 : chunk * FIELDS] = increment.reshape(chunk * FIELDS, padded, cycle)[:, :rows]

    each = groups // turns

    def send_back(turn):
        def repack(group, carry):
            for tile in range(cycle // LANES):
                parts = [result[4 * group + j, :, tile * LANES : (tile + 1) * LANES] for j in range(4)]
                for m, value in enumerate(block_transpose(parts, cols)):
                    outgoing[4 * tile + m, turn * each + group] = value
            return carry

        lax.fori_loop(0, each, repack, 0)
        part = pl.ds(turn * each, each)
        keep_back = pltpu.make_async_copy(
            outgoing.at[me, part], out_ref.at[me, part], back_send.at[turn, 0]
        )
        keep_back.start()
        backs = [keep_back]
        for k in range(1, wide_count):
            peer = lax.rem(me + k, wide_count)
            copy = pltpu.make_async_remote_copy(
                src_ref=outgoing.at[peer, part],
                dst_ref=out_ref.at[me, part],
                send_sem=back_send.at[turn, k],
                recv_sem=back_recv.at[turn, k],
                device_id=(peer, band),
                device_id_type=MESH,
            )
            copy.start()
            backs.append(copy)
        return backs

    def compute(turn):
        up_copy, down_copy = halo_copies(turn)

        @pl.when(has_below)
        def _():
            up_copy.wait_recv()

        @pl.when(has_above)
        def _():
            down_copy.wait_recv()

        lax.fori_loop(turn * chunk, (turn + 1) * chunk, take_halo, 0)
        sweep(turn)
        return send_back(turn)

    keep.wait()
    backs = []
    for turn in range(turns):
        for k in range(1, wide_count):
            sends[turn][k].wait_recv()
        lax.fori_loop(turn * chunk, (turn + 1) * chunk, unpack, 0)
        up_copy, down_copy = halo_copies(turn)

        @pl.when(has_above)
        def _():
            up_copy.start()

        @pl.when(has_below)
        def _():
            down_copy.start()

        if turn > 0:
            backs += compute(turn - 1)
    backs += compute(turns - 1)

    for turn in range(turns):
        for k in range(1, wide_count):
            sends[turn][k].wait_send()
        up_copy, down_copy = halo_copies(turn)

        @pl.when(has_above)
        def _():
            up_copy.wait_send()

        @pl.when(has_below)
        def _():
            down_copy.wait_send()

    for copy in backs:
        copy.wait()


def finish_kernel(chunk, traj_ref, inc_ref, spread_ref, out_ref, tall):
    fields, levels, fine_rows, fine_cols = traj_ref.shape
    groups, rows = inc_ref.shape[1:3]
    part = inc_ref[0].reshape(groups * rows, LANES)
    for t in range(COARSEN):
        tall[pl.ds(t, groups * rows, stride=COARSEN), :] = part
    each = groups // (levels // chunk)
    for turn in range(levels // chunk):
        span = each * fine_rows
        operand = jnp.concatenate(split_bf16(tall[turn * span : (turn + 1) * span]), axis=1)
        wide = dot(operand, spread_ref[...])
        for place in range(chunk * fields):
            level, f = divmod(turn * chunk * fields + place, fields)
            group, j = divmod(place, 4)
            fine = wide[group * fine_rows : (group + 1) * fine_rows, j * LANES : (j + 1) * LANES]
            out_ref[f, level] = (traj_ref[f, level].astype(jnp.float32) + fine).astype(jnp.bfloat16)


def shards(trajectory, innovation, background, obs_weight):
    wide_count = lax.axis_size("wide")
    narrow_count = lax.axis_size("narrow")
    narrow_index = lax.axis_index("narrow")
    fields, total_levels, rows, cols = innovation.shape
    fine_rows, fine_cols = trajectory.shape[2:]
    cycle = cols * wide_count
    total_rows = rows * narrow_count
    levels = -(-total_levels // wide_count)
    last = -(-total_levels // levels) - 1
    chunk = max(c for c in range(1, 6) if levels % c == 0)
    packed = ITEMS // 4
    turns = levels // chunk
    groups = turns * -(-fields * chunk // 4)
    padded = rows + 2 * HALO

    lane = np.arange(fine_cols)
    pool = np.zeros((fine_cols, LANES), np.float32)
    pool[lane, FIELDS % 4 * cols + lane // COARSEN] = 1.0
    spread = np.zeros((LANES, 4 * LANES), np.float32)
    for j in range(4):
        spread[j * cols + lane // COARSEN, j * LANES + lane] = 1.0
    pool = jnp.asarray(pool, jnp.bfloat16)
    spread = jnp.asarray(np.concatenate([spread, spread]), jnp.bfloat16)

    sent = pl.pallas_call(
        pack_kernel,
        grid=(rows // 8,),
        in_specs=[
            pl.BlockSpec((1, total_levels, 8 * COARSEN, fine_cols), lambda r: (0, 0, r, 0)),
            pl.BlockSpec((fields, 8, cols, total_levels), lambda r: (0, r, 0, 0)),
            pl.BlockSpec((fields, 8, cols, total_levels), lambda r: (0, r, 0, 0)),
            pl.BlockSpec((8, cols, total_levels), lambda r: (r, 0, 0)),
            pl.BlockSpec((fine_cols, LANES), lambda r: (0, 0)),
        ],
        out_specs=pl.BlockSpec((total_levels, packed, 8, LANES), lambda r: (0, 0, r, 0)),
        out_shape=jax.ShapeDtypeStruct((wide_count * levels, packed, rows, LANES), jnp.float32),
        scratch_shapes=[pltpu.VMEM((total_levels * 8 * COARSEN, LANES), jnp.float32)],
        name="pack",
    )(
        trajectory,
        innovation.transpose(0, 2, 3, 1),
        background.transpose(0, 2, 3, 1),
        obs_weight.transpose(1, 2, 0),
        pool,
    )
    sent = sent.reshape(wide_count, levels * packed, rows, LANES)

    place = jnp.arange(padded, dtype=jnp.int32)
    row_index = jnp.where(place < rows + HALO, place, place - padded) + narrow_index * rows
    wavenumber = jnp.arange(cycle, dtype=jnp.int32)
    folded = jnp.minimum(wavenumber, cycle - wavenumber).astype(jnp.float32)
    latitude = jnp.pi * ((row_index.astype(jnp.float32) + 0.5) / total_rows - 0.5)
    cutoff = 0.5 * cycle * jnp.cos(latitude)
    inside = (row_index >= 0) & (row_index < total_rows)
    cutoff = jnp.where(inside, cutoff, 1.0)
    response = 1.0 / (1.0 + (folded[None, :] / cutoff[:, None]) ** 4)
    response = jnp.where(inside[:, None], response, 0.0) / cycle

    phase = np.arange(cycle)[:, None] * np.arange(cycle)[None, :] % cycle
    wave = np.cos(2.0 * np.pi / cycle * phase) + np.sin(2.0 * np.pi / cycle * phase)
    wave = wave.astype(np.float32)
    wave_high = wave.astype(jnp.bfloat16)
    wave_low = (wave - wave_high.astype(np.float32)).astype(jnp.bfloat16)

    vmem = pl.BlockSpec(memory_space=pltpu.VMEM)
    anywhere = pl.BlockSpec(memory_space=pl.ANY)
    f32 = jnp.float32
    moved_back = pl.pallas_call(
        functools.partial(sweep_kernel, wide_count, narrow_count, levels, chunk),
        in_specs=[anywhere, vmem, vmem, vmem],
        out_specs=anywhere,
        out_shape=jax.ShapeDtypeStruct((wide_count, groups, rows, LANES), f32),
        scratch_shapes=[
            pltpu.VMEM((wide_count, levels * packed, rows, LANES), f32),
            pltpu.VMEM((levels * ITEMS, padded, cycle), f32),
            pltpu.VMEM((groups // turns * 4, rows, cycle), f32),
            pltpu.VMEM((wide_count, groups, rows, LANES), f32),
            pltpu.VMEM((levels * ITEMS, 8, cycle // 2), f32),
            pltpu.VMEM((levels * ITEMS, 8, cycle // 2), f32),
            pltpu.VMEM((levels * ITEMS, 8, cycle // 2), f32),
            pltpu.VMEM((levels * ITEMS, 8, cycle // 2), f32),
            pltpu.SemaphoreType.DMA((1,)),
            pltpu.SemaphoreType.DMA((turns, wide_count)),
            pltpu.SemaphoreType.DMA((turns, wide_count)),
            pltpu.SemaphoreType.DMA((turns, 2)),
            pltpu.SemaphoreType.DMA((turns, 2)),
            pltpu.SemaphoreType.DMA((turns, wide_count)),
            pltpu.SemaphoreType.DMA((turns, wide_count)),
        ],
        compiler_params=pltpu.CompilerParams(
            collective_id=0, has_side_effects=True, vmem_limit_bytes=32 * 1024 * 1024
        ),
        name="sweep",
    )(sent, response, jnp.asarray(wave_high), jnp.asarray(wave_low))

    return pl.pallas_call(
        functools.partial(finish_kernel, chunk),
        grid=(last + 1,),
        in_specs=[
            pl.BlockSpec((fields, levels, fine_rows, fine_cols), lambda s: (0, s, 0, 0)),
            pl.BlockSpec((1, groups, rows, LANES), lambda s: (s, 0, 0, 0)),
            pl.BlockSpec((2 * LANES, 4 * LANES), lambda s: (0, 0)),
        ],
        out_specs=pl.BlockSpec((fields, levels, fine_rows, fine_cols), lambda s: (0, s, 0, 0)),
        out_shape=jax.ShapeDtypeStruct(trajectory.shape, jnp.bfloat16),
        scratch_shapes=[
            pltpu.VMEM((groups * fine_rows, LANES), f32),
        ],
        compiler_params=pltpu.CompilerParams(vmem_limit_bytes=32 * 1024 * 1024),
        name="finish",
    )(trajectory, moved_back, spread)


def solution(mesh):
    in_specs = (
        P(None, None, "narrow", "wide"),
        P(None, None, "narrow", "wide"),
        P(None, None, "narrow", "wide"),
        P(None, "narrow", "wide"),
    )
    out_specs = P(None, None, "narrow", "wide")
    return jax.shard_map(shards, mesh=mesh, in_specs=in_specs, out_specs=out_specs, check_vma=False)
```
